256 devices in a mesh: seq: 32 (over x_lo, z, core), batch: 8 (over y, x_hi).
Axes of the slice: x: 4 (x_hi: 2, x_lo: 2; x = x_hi * 2 + x_lo), y: 4, z: 8, core: 2. Of those that a mesh axis runs over, the one named last changes fastest.
Arguments:
- queries: bfloat16 [65536, 2048], P(('batch', 'seq')), parts along dimension 0, may hold values from -9 to 9
- key_rows: bfloat16 [65536, 2048], P(('batch', 'seq')), parts along dimension 0, may hold values from -9 to 9
- values: bfloat16 [65536, 2048], P(('batch', 'seq')), parts along dimension 0, may hold values from -6 to 6
- bias_tiles: bfloat16 [3, 256, 256], replicated, may hold values from -6 to 6
- buckets: int32 [5], replicated, may hold values from 0 to 2
- slopes: float32 [32], replicated, may hold values from 0.3 to 1.5
Outputs:
- attended: bfloat16 [65536, 2048], P(('batch', 'seq')), parts along dimension 0
The draws below stay inside these ranges and needn't reach their ends.
There are 8 independent parts, one for each index of `batch`. The reference program is written for one: setup_inputs(seed, part) draws one part's arguments, and reference() takes and returns one part's arrays. A program takes and returns all parts, laid end to end along the dimension named above; an argument that names none is the same for every part. Nothing has to cross between parts.
All inputs are finite; a program needn't handle non-finite values.
Results may differ from the reference program's by a relative error of at most 0.0043.
Values may be sent and summed in bfloat16 or wider, within the bound.
A program may use at most 128 MiB of HBM per device.

```python
import math
import jax
import jax.numpy as jnp
from jax import lax

H = 32
HD = 64
TOK_DEV = 256
WIN = 4
NBUCKET = 3
D = 2048
LEN = 8192


def base_draw(key, salt):
    return jnp.clip(jax.random.normal(jax.random.fold_in(key, salt), (LEN, H * HD), jnp.float32), -6.0, 6.0)


def draw_queries(key, part):
    result = base_draw(key, 1)
    return result.astype(jnp.bfloat16)


def draw_key_rows(key, part):
    result = base_draw(key, 2)
    return result.astype(jnp.bfloat16)


def with_ends(values, own_key, low, largest):
    spot = [jax.random.randint(jax.random.fold_in(own_key, axis), (), 0, length) for axis, length in enumerate(values.shape)]
    longest = values.shape.index(max(values.shape))
    beside = spot[:longest] + [(spot[longest] + 1) % values.shape[longest]] + spot[longest + 1:]
    return values.at[tuple(spot)].set(low).at[tuple(beside)].set(largest)


def shard_levels(own_key, dims, split, smallest, high):
    def one(position, shards_of):
        draws = jax.random.uniform(jax.random.fold_in(jax.random.fold_in(own_key, 6), position), (shards_of,), jnp.float32, smallest / len(split), high / len(split))
        return jnp.repeat(jnp.exp(draws), dims[position] // shards_of).reshape((-1,) + (1,) * (len(dims) - position - 1))

    level = one(*split[0])
    for cut in split[1:]:
        level = level * one(*cut)
    return level


def normal_values(key, extent, width, most, split=(), held_as=jnp.bfloat16):
    array = jax.random.normal(key, extent, jnp.float32) * width
    if len(split) > 0:
        array = shard_levels(key, extent, split, -0.22, 0.18) * array
    return jnp.clip(array, min=-most, max=most).astype(held_as)


def setup_inputs(seed: int = 0, part: int = 0) -> dict:
    key_list = jax.random.split(jax.random.key(seed), 7)
    part_splits = jax.random.split(jax.random.fold_in(key_list[6], part), 7)
    queries = draw_queries(jax.random.fold_in(jax.random.fold_in(key_list[6], part), 71), part)
    key_rows = draw_key_rows(jax.random.fold_in(jax.random.fold_in(key_list[6], part), 71), part)
    values = normal_values(part_splits[2], (LEN, D), 1.0, 6.0, ((0, 32),))
    bias_tiles = normal_values(key_list[3], (NBUCKET, TOK_DEV, TOK_DEV), 1.0, 6.0)
    buckets = with_ends(jax.random.randint(key_list[4], (WIN + 1,), 0, NBUCKET), jax.random.fold_in(key_list[4], 1), 0, NBUCKET - 1).astype(jnp.int32)
    slopes = jnp.clip(jnp.exp(jax.random.uniform(key_list[5], (H,), jnp.float32, math.log(0.3), math.log(1.5))), 0.3, 1.5)
    return dict(queries=queries, key_rows=key_rows, values=values, bias_tiles=bias_tiles, buckets=buckets, slopes=slopes)


def window_bias(bias_tiles, buckets):
    pieces = []
    for offset in range(-WIN, WIN + 1):
        tile = bias_tiles[buckets[abs(offset)]].astype(jnp.float32)
        if offset < 0:
            tile = tile.T
        pieces.append(tile)
    return jnp.concatenate(pieces, axis=1)


def block_attention(query_part, key_part, value_part, bias_window, slope_part):
    head_count = slope_part.shape[0]
    head_width = query_part.shape[1] // head_count
    group_size = min(head_count, 4)
    group_count = head_count // group_size
    row_count = query_part.shape[0]
    key_count = key_part.shape[0]
    query_groups = query_part.reshape(row_count, group_count, group_size, head_width).transpose(1, 0, 2, 3)
    key_groups = key_part.reshape(key_count, group_count, group_size, head_width).transpose(1, 0, 2, 3)
    value_groups = value_part.reshape(key_count, group_count, group_size, head_width).transpose(1, 0, 2, 3)
    slope_groups = slope_part.reshape(group_count, group_size)

    def per_group(packed):
        query_one, key_one, value_one, slope_one = packed
        scores = jnp.einsum("qgd,kgd->gqk", query_one.astype(jnp.float32), key_one.astype(jnp.float32))
        scores = scores * (HD ** -0.5) + slope_one.astype(jnp.float32)[:, None, None] * bias_window[None]
        peaks = jnp.max(scores, axis=-1, keepdims=True)
        raised = jnp.exp(scores - peaks)
        totals = jnp.sum(raised, axis=-1)
        weights = lax.optimization_barrier(raised.astype(jnp.bfloat16))
        weighted = jnp.einsum("gqk,kgd->qgd", weights.astype(jnp.float32), value_one.astype(jnp.float32))
        return (weighted / totals.T[:, :, None]).astype(jnp.bfloat16)

    results = lax.map(per_group, (query_groups, key_groups, value_groups, slope_groups))
    return results.transpose(1, 0, 2, 3).reshape(row_count, head_count * head_width)


def reference(queries, key_rows, values, bias_tiles, buckets, slopes):
    bias_window = window_bias(bias_tiles, buckets)
    block_total = queries.shape[0] // TOK_DEV
    width_all = queries.shape[1]
    key_blocks = key_rows.reshape(block_total, TOK_DEV, width_all)
    value_blocks = values.reshape(block_total, TOK_DEV, width_all)
    offsets = jnp.arange(-WIN, WIN + 1, dtype=jnp.int32)

    def per_block(block):
        query_part = lax.dynamic_slice_in_dim(queries, (block * TOK_DEV).astype(jnp.int32), TOK_DEV, 0)
        chosen = ((block + offsets) % block_total).astype(jnp.int32)
        key_part = key_blocks[chosen].reshape(-1, width_all)
        value_part = value_blocks[chosen].reshape(-1, width_all)
        return block_attention(query_part, key_part, value_part, bias_window, slopes)

    results = lax.map(per_block, jnp.arange(block_total, dtype=jnp.int32))
    return results.reshape(block_total * TOK_DEV, width_all)
```

```python
import functools
import math

import jax
import jax.numpy as jnp
from jax import lax
from jax.experimental import pallas as pl
from jax.experimental.pallas import tpu as pltpu
from jax.sharding import PartitionSpec as P

MESH = pl.DeviceIdType.MESH
HD = 64
WIN = 4
LANES = 128
LOG2E = math.log2(math.e)
AHEAD = 2

OWN, SIB, A_LOW, A_HIGH, B_LOW, B_HIGH, C_LOW, C_HIGH, FAR = range(9)
NEAR = (OWN, SIB, A_LOW, A_HIGH, B_LOW, B_HIGH)
OUTER = (C_LOW, C_HIGH, FAR)


def kernel(
    ring, buckets, slopes, q_hbm, k_hbm, v_hbm, tiles_hbm, out_ref,
    kv, q_buf, tiles, bias, send_sem, recv_sem, in_sem,
):
    groups, rows = kv.shape[0], kv.shape[3]
    me = lax.axis_index("seq")
    core = lax.rem(me, 2)
    up = lax.rem(me + 2, ring)
    down = lax.rem(me + ring - 2, ring)
    sib = me + 1 - 2 * core

    def columns(g):
        return pl.ds(pl.multiple_of(g * LANES, LANES), LANES)

    def remote(src, dst_slot, g, target):
        return pltpu.make_async_remote_copy(
            src_ref=src,
            dst_ref=kv.at[g, dst_slot],
            send_sem=send_sem.at[dst_slot, g],
            recv_sem=recv_sem.at[dst_slot, g],
            device_id={"seq": target},
            device_id_type=MESH,
        )

    def send_own(g, dst_slot, target):
        for part, ref in enumerate((k_hbm, v_hbm)):
            pltpu.make_async_remote_copy(
                src_ref=ref.at[:, columns(g)],
                dst_ref=kv.at[g, dst_slot, part],
                send_sem=send_sem.at[dst_slot, g],
                recv_sem=recv_sem.at[dst_slot, g],
                device_id={"seq": target},
                device_id_type=MESH,
            ).start()

    def send_own_all(g):
        send_own(g, A_LOW, up)
        send_own(g, A_HIGH, down)
        send_own(g, SIB, sib)

    def arrived(slot, g):
        remote(kv.at[g, slot], slot, g, sib).wait_recv()

    def forward(g):
        arrived(A_LOW, g)
        remote(kv.at[g, A_LOW], C_LOW, g, up).start()
        remote(kv.at[g, A_LOW], B_LOW, g, sib).start()
        arrived(A_HIGH, g)
        remote(kv.at[g, A_HIGH], C_HIGH, g, down).start()
        remote(kv.at[g, A_HIGH], B_HIGH, g, sib).start()

    barrier = pltpu.get_barrier_semaphore()
    for target in (up, down, sib):
        pl.semaphore_signal(barrier, inc=1, device_id={"seq": target}, device_id_type=MESH)
    pl.semaphore_wait(barrier, 3)

    for g in range(AHEAD):
        send_own_all(g)

    tiles_copy = pltpu.make_async_copy(tiles_hbm, tiles, in_sem.at[0])
    tiles_copy.start()

    @pl.loop(0, groups)
    def _(g):
        pltpu.make_async_copy(q_hbm.at[:, columns(g)], q_buf.at[g], in_sem.at[1]).start()
        pltpu.make_async_copy(k_hbm.at[:, columns(g)], kv.at[g, OWN, 0], in_sem.at[2]).start()
        pltpu.make_async_copy(v_hbm.at[:, columns(g)], kv.at[g, OWN, 1], in_sem.at[2]).start()

    tiles_copy.wait()
    for o in range(WIN + 1):
        tile = tiles[buckets[o]].astype(jnp.float32)
        bias[WIN + o] = tile
        if o > 0:
            bias[WIN - o] = tile.T
    pltpu.make_async_copy(q_buf, q_buf, in_sem.at[1]).wait()
    pltpu.make_async_copy(kv.at[:, OWN], kv.at[:, OWN], in_sem.at[2]).wait()

    offset = {
        OWN: 0,
        SIB: 1 - 2 * core,
        A_LOW: -2,
        A_HIGH: 2,
        B_LOW: -1 - 2 * core,
        B_HIGH: 3 - 2 * core,
        C_LOW: -4,
        C_HIGH: 4,
        FAR: 6 * core - 3,
    }
    lane_head = lax.broadcasted_iota(jnp.int32, (1, LANES), 1) // HD

    def scores(g, query, slope, slots):
        result = []
        for slot in slots:
            dots = lax.dot_general(
                query, kv[g, slot, 0], (((1,), (1,)), ((), ())),
                preferred_element_type=jnp.float32,
            )
            result.append(dots * LOG2E + slope * bias[offset[slot] + WIN])
        return result

    def row_max(parts):
        return jnp.max(functools.reduce(jnp.maximum, parts), axis=1, keepdims=True)

    def weighted(g, parts, peak, half, slots):
        total = None
        for part, slot in zip(parts, slots):
            weights = jnp.exp2(part - peak).astype(jnp.bfloat16)
            value = jnp.where(lane_head == half, kv[g, slot, 1], jnp.ones((), jnp.bfloat16))
            term = jnp.dot(weights, value, preferred_element_type=jnp.float32)
            total = term if total is None else total + term
        return total

    forward(0)

    @pl.loop(0, groups)
    def _(g):
        @pl.when(g + AHEAD < groups)
        def _():
            send_own_all(g + AHEAD)

        @pl.when(g + 1 < groups)
        def _():
            forward(g + 1)

        for slot in (SIB, B_LOW, B_HIGH):
            arrived(slot, g)
        query = q_buf[g] * jnp.asarray(HD ** -0.5, jnp.bfloat16)
        queries, slope, peaks, sums = [], [], [], []
        for half in range(2):
            queries.append(jnp.where(lane_head == half, query, jnp.zeros((), jnp.bfloat16)))
            slope.append(slopes[2 * g + half] * LOG2E)
            parts = scores(g, queries[half], slope[half], NEAR)
            peaks.append(row_max(parts))
            sums.append(weighted(g, parts, peaks[half], half, NEAR))

        mine = C_HIGH - core
        arrived(mine, g)
        remote(kv.at[g, mine], FAR, g, sib).start()
        arrived(C_LOW + core, g)
        arrived(FAR, g)
        totals = []
        for half in range(2):
            parts = scores(g, queries[half], slope[half], OUTER)
            peak = jnp.maximum(peaks[half], row_max(parts))
            totals.append(
                sums[half] * jnp.exp2(peaks[half] - peak)
                + weighted(g, parts, peak, half, OUTER)
            )
        first = lane_head == 0
        top = jnp.where(first, totals[0], totals[1])
        low = pltpu.roll(jnp.where(first, totals[1], totals[0]), HD, 1)
        out_ref[:, columns(g)] = (top / low).astype(out_ref.dtype)

    for slot, target in (
        (SIB, sib), (A_LOW, up), (A_HIGH, down), (B_LOW, sib), (B_HIGH, sib),
        (C_LOW, up), (C_HIGH, down), (FAR, sib),
    ):
        @pl.loop(0, groups)
        def _(g):
            remote(kv.at[g, slot], slot, g, target).wait_send()


def solution(mesh):
    ring = mesh.shape["seq"]

    def per_device(queries, key_rows, values, bias_tiles, buckets, slopes):
        rows, width = queries.shape
        groups = width // LANES
        return pl.pallas_call(
            functools.partial(kernel, ring),
            out_shape=jax.ShapeDtypeStruct((rows, width), queries.dtype),
            in_specs=[pl.BlockSpec(memory_space=pltpu.SMEM)] * 2
            + [pl.BlockSpec(memory_space=pl.ANY)] * 4,
            out_specs=pl.BlockSpec(memory_space=pltpu.VMEM),
            scratch_shapes=[
                pltpu.VMEM((groups, 9, 2, rows, LANES), jnp.bfloat16),
                pltpu.VMEM((groups, rows, LANES), jnp.bfloat16),
                pltpu.VMEM(bias_tiles.shape, jnp.bfloat16),
                pltpu.VMEM((2 * WIN + 1, rows, rows), jnp.float32),
                pltpu.SemaphoreType.DMA((9, groups)),
                pltpu.SemaphoreType.DMA((9, groups)),
                pltpu.SemaphoreType.DMA((3,)),
            ],
            compiler_params=pltpu.CompilerParams(
                collective_id=0, has_side_effects=True, vmem_limit_bytes=56 << 20
            ),
        )(buckets, slopes, queries, key_rows, values, bias_tiles)

    return jax.shard_map(
        per_device,
        mesh=mesh,
        in_specs=(P(("batch", "seq"), None),) * 3 + (P(), P(), P()),
        out_specs=P(("batch", "seq"), None),
        check_vma=False,
    )
```

```python
import functools
import math

import jax
import jax.numpy as jnp
from jax import lax
from jax.experimental import pallas as pl
from jax.experimental.pallas import tpu as pltpu
from jax.sharding import PartitionSpec as P

MESH = pl.DeviceIdType.MESH
HD = 64
WIN = 4
LANES = 128
PACK = 16
LOG2E = math.log2(math.e)

OWN, SIB, A_LOW, A_HIGH, B_LOW, B_HIGH, C_LOW, C_HIGH, FAR = range(9)
NEAR = (OWN, SIB, A_LOW, A_HIGH, B_LOW, B_HIGH)
OUTER = (C_LOW, C_HIGH, FAR)


def kernel(
    ring, buckets, slopes, q_hbm, k_hbm, v_hbm, tiles_hbm, out_ref,
    kv, q_buf, k_buf, v_buf, tiles, bias, state, send_sem, recv_sem, in_sem,
):
    groups, rows = kv.shape[1], q_buf.shape[0]
    pieces = rows // PACK
    me = lax.axis_index("seq")
    core = lax.rem(me, 2)
    up = lax.rem(me + 2, ring)
    down = lax.rem(me + ring - 2, ring)
    sib = me + 1 - 2 * core

    def columns(g):
        return pl.ds(pl.multiple_of(g * LANES, LANES), LANES)

    def copy(src, dst, g, target):
        return pltpu.make_async_remote_copy(
            src_ref=kv.at[src, g],
            dst_ref=kv.at[dst, g],
            send_sem=send_sem.at[dst, g],
            recv_sem=recv_sem.at[dst, g],
            device_id={"seq": target},
            device_id_type=MESH,
        )

    def arrived(slot, g):
        copy(slot, slot, g, sib).wait_recv()

    loads = [
        pltpu.make_async_copy(src, dst, in_sem.at[i])
        for i, (src, dst) in enumerate(
            ((k_hbm, k_buf), (v_hbm, v_buf), (tiles_hbm, tiles), (q_hbm, q_buf))
        )
    ]
    for load in loads:
        load.start()

    barrier = pltpu.get_barrier_semaphore()
    for target in (up, down, sib):
        pl.semaphore_signal(barrier, inc=1, device_id={"seq": target}, device_id_type=MESH)
    pl.semaphore_wait(barrier, 3)
    loads[0].wait()
    loads[1].wait()

    @pl.loop(0, groups)
    def _(g):
        for half, buf in enumerate((k_buf, v_buf)):
            block = buf[:, columns(g)]
            for j in range(pieces):
                at = (half * pieces + j) * LANES
                kv[OWN, g, :, at : at + LANES] = block[j * PACK : (j + 1) * PACK]
        copy(OWN, A_LOW, g, up).start()
        copy(OWN, A_HIGH, g, down).start()
        copy(OWN, SIB, g, sib).start()

    def forward(g):
        arrived(A_LOW, g)
        copy(A_LOW, C_LOW, g, up).start()
        copy(A_LOW, B_LOW, g, sib).start()
        arrived(A_HIGH, g)
        copy(A_HIGH, C_HIGH, g, down).start()
        copy(A_HIGH, B_HIGH, g, sib).start()

    def share(g):
        mine = C_HIGH - core
        arrived(mine, g)
        copy(mine, FAR, g, sib).start()

    loads[2].wait()
    for o in range(WIN + 1):
        tile = tiles[buckets[o]].astype(jnp.float32)
        bias[WIN + o] = tile
        if o > 0:
            bias[WIN - o] = tile.T
    loads[3].wait()

    offset = {
        OWN: 0,
        SIB: 1 - 2 * core,
        A_LOW: -2,
        A_HIGH: 2,
        B_LOW: -1 - 2 * core,
        B_HIGH: 3 - 2 * core,
        C_LOW: -4,
        C_HIGH: 4,
        FAR: 6 * core - 3,
    }
    lane_head = lax.broadcasted_iota(jnp.int32, (1, LANES), 1) // HD
    first = lane_head == 0

    def block(slot, g, half):
        span = pieces * LANES
        packed = kv[slot, g, :, half * span : (half + 1) * span]
        return jnp.concatenate(
            [packed[:, j * LANES : (j + 1) * LANES] for j in range(pieces)], axis=0
        )

    def attend(g, slots):
        query = q_buf[:, columns(g)] * jnp.asarray(HD ** -0.5, jnp.bfloat16)
        totals, peaks = [], []
        for half in range(2):
            mask = lane_head == half
            chosen = jnp.where(mask, query, jnp.zeros((), jnp.bfloat16))
            slope = slopes[2 * g + half] * LOG2E
            scores = []
            for slot in slots:
                dots = lax.dot_general(
                    chosen, block(slot, g, 0), (((1,), (1,)), ((), ())),
                    preferred_element_type=jnp.float32,
                )
                scores.append(dots * LOG2E + slope * bias[offset[slot] + WIN])
            peak = jnp.max(functools.reduce(jnp.maximum, scores), axis=1, keepdims=True)
            total = None
            for score, slot in zip(scores, slots):
                weights = jnp.exp2(score - peak).astype(jnp.bfloat16)
                value = jnp.where(mask, block(slot, g, 1), jnp.ones((), jnp.bfloat16))
                term = jnp.dot(weights, value, preferred_element_type=jnp.float32)
                total = term if total is None else total + term
            totals.append(total)
            peaks.append(peak)
        top = jnp.where(first, totals[0], totals[1])
        low = pltpu.roll(jnp.where(first, totals[1], totals[0]), HD, 1)
        return top, low, jnp.where(first, peaks[0], peaks[1])

    forward(0)

    @pl.loop(0, groups)
    def _(g):
        @pl.when(g + 1 < groups)
        def _():
            forward(g + 1)

        for slot in (SIB, B_LOW, B_HIGH):
            arrived(slot, g)
        for i, value in enumerate(attend(g, NEAR)):
            state[g, i] = value

    share(0)

    @pl.loop(0, groups)
    def _(g):
        @pl.when(g + 1 < groups)
        def _():
            share(g + 1)

        arrived(C_LOW + core, g)
        arrived(FAR, g)
        top, low, peak = attend(g, OUTER)
        best = jnp.maximum(peak, state[g, 2])
        new, old = jnp.exp2(peak - best), jnp.exp2(state[g, 2] - best)
        result = (top * new + state[g, 0] * old) / (low * new + state[g, 1] * old)
        out_ref[:, columns(g)] = result.astype(out_ref.dtype)

    for slot, target in (
        (SIB, sib), (A_LOW, up), (A_HIGH, down), (B_LOW, sib), (B_HIGH, sib),
        (C_LOW, up), (C_HIGH, down), (FAR, sib),
    ):
        @pl.loop(0, groups)
        def _(g):
            copy(slot, slot, g, target).wait_send()


def solution(mesh):
    ring = mesh.shape["seq"]

    def per_device(queries, key_rows, values, bias_tiles, buckets, slopes):
        rows, width = queries.shape
        groups = width // LANES
        return pl.pallas_call(
            functools.partial(kernel, ring),
            out_shape=pltpu.VMEM((rows, width), queries.dtype),
            in_specs=[pl.BlockSpec(memory_space=pltpu.SMEM)] * 2
            + [pl.BlockSpec(memory_space=pl.ANY)] * 4,
            out_specs=pl.BlockSpec(memory_space=pltpu.VMEM),
            scratch_shapes=[
                pltpu.VMEM((9, groups, PACK, 2 * LANES * rows // PACK), jnp.bfloat16),
                pltpu.VMEM((rows, width), jnp.bfloat16),
                pltpu.VMEM((rows, width), jnp.bfloat16),
                pltpu.VMEM((rows, width), jnp.bfloat16),
                pltpu.VMEM(bias_tiles.shape, jnp.bfloat16),
                pltpu.VMEM((2 * WIN + 1, rows, rows), jnp.float32),
                pltpu.VMEM((groups, 3, rows, LANES), jnp.float32),
                pltpu.SemaphoreType.DMA((9, groups)),
                pltpu.SemaphoreType.DMA((9, groups)),
                pltpu.SemaphoreType.DMA((4,)),
            ],
            compiler_params=pltpu.CompilerParams(
                collective_id=0, has_side_effects=True, vmem_limit_bytes=56 << 20
            ),
        )(buckets, slopes, queries, key_rows, values, bias_tiles)

    return jax.shard_map(
        per_device,
        mesh=mesh,
        in_specs=(P(("batch", "seq"), None),) * 3 + (P(), P(), P()),
        out_specs=P(("batch", "seq"), None),
        check_vma=False,
    )
```

```python
import functools
import math

import jax
import jax.numpy as jnp
from jax import lax
from jax.experimental import pallas as pl
from jax.experimental.pallas import tpu as pltpu
from jax.sharding import PartitionSpec as P

MESH = pl.DeviceIdType.MESH
HD = 64
WIN = 4
LANES = 128
LOG2E = math.log2(math.e)

OWN, SIB, A_LOW, A_HIGH, B_LOW, B_HIGH, C_LOW, C_HIGH, FAR = range(9)


def kernel(
    ring, buckets_hbm, slopes_hbm, q_hbm, k_hbm, v_hbm, tiles_hbm, out_ref,
    kv, q_buf, tiles, bias, state, buckets, slopes, send_sem, recv_sem, in_sem,
):
    groups = q_buf.shape[1] // LANES
    me = lax.axis_index("seq")
    core = lax.rem(me, 2)
    up = lax.rem(me + 2, ring)
    down = lax.rem(me + ring - 2, ring)
    sib = me + 1 - 2 * core
    own_chunks = spans(groups, (4, 4, 4))
    far_chunks = spans(groups, (4, 4, 2, 2, 1, 1, 1))
    target = (lax.rem(me + ring - 2 + 4 * core, ring), lax.rem(me + 2 + ring - 4 * core, ring))
    near_slot = (A_HIGH - core, A_LOW + core)
    sib_slot = (B_HIGH - core, B_LOW + core)
    far_slot = (C_HIGH - core, C_LOW + core)

    def columns(g, count=1):
        return pl.ds(pl.multiple_of(g * LANES, LANES), count * LANES)

    def remote(src, slot, chunk, part, i, device):
        return pltpu.make_async_remote_copy(
            src_ref=src.at[:, columns(*chunk)],
            dst_ref=kv.at[slot, part, :, columns(*chunk)],
            send_sem=send_sem.at[slot, part, i],
            recv_sem=recv_sem.at[slot, part, i],
            device_id={"seq": device},
            device_id_type=MESH,
        )

    def send_own(i, slot, device):
        for part, ref in enumerate((k_hbm, v_hbm)):
            remote(ref, slot, own_chunks[i], part, i, device).start()

    def pass_on(src, slot, chunks, i, device):
        for part in range(2):
            remote(kv.at[src, part], slot, chunks[i], part, i, device).start()

    def arrived(slot, chunks, i):
        for part in range(2):
            remote(kv.at[slot, part], slot, chunks[i], part, i, sib).wait_recv()

    def signal(semaphore, device):
        pl.semaphore_signal(semaphore, inc=1, device_id={"seq": device}, device_id_type=MESH)

    loads = [
        pltpu.make_async_copy(src, dst, in_sem.at[i])
        for i, (src, dst) in enumerate((
            (buckets_hbm, buckets), (tiles_hbm, tiles), (slopes_hbm, slopes), (q_hbm, q_buf),
            (k_hbm, kv.at[OWN, 0]), (v_hbm, kv.at[OWN, 1]),
        ))
    ]
    barrier = pltpu.get_barrier_semaphore()
    for device in (up, down, sib):
        signal(barrier, device)
    for load in loads:
        load.start()
    pl.semaphore_wait(barrier, 3)

    def start_stream(stream):
        for i in range(len(own_chunks)):
            send_own(i, near_slot[stream], target[stream])

    start_stream(0)
    for i in range(len(own_chunks)):
        send_own(i, SIB, sib)

    loads[0].wait()
    loads[1].wait()
    for o in range(WIN + 1):
        tile = tiles[buckets[o]].astype(jnp.float32)
        bias[WIN + o] = tile
        if o > 0:
            bias[WIN - o] = tile.T

    remote(k_hbm, near_slot[0], own_chunks[0], 0, 0, sib).wait_send()
    start_stream(1)
    for load in loads[2:]:
        load.wait()

    lane_head = lax.broadcasted_iota(jnp.int32, (1, LANES), 1) // HD
    first = lane_head == 0
    near = (
        (OWN, 0), (SIB, 1 - 2 * core), (A_LOW, -2), (A_HIGH, 2),
        (B_LOW, -1 - 2 * core), (B_HIGH, 3 - 2 * core),
    )
    outer = ((C_LOW, -4), (C_HIGH, 4), (FAR, 6 * core - 3))

    def attend(g, blocks):
        query = q_buf[:, columns(g)] * jnp.asarray(HD ** -0.5, jnp.bfloat16)
        totals, peaks = [], []
        for half in range(2):
            mask = lane_head == half
            chosen = jnp.where(mask, query, jnp.zeros((), jnp.bfloat16))
            slope = slopes[2 * g + half] * LOG2E
            scores = []
            for slot, offset in blocks:
                dots = lax.dot_general(
                    chosen, kv[slot, 0, :, columns(g)], (((1,), (1,)), ((), ())),
                    preferred_element_type=jnp.float32,
                )
                scores.append(dots * LOG2E + slope * bias[offset + WIN])
            peak = jnp.max(functools.reduce(jnp.maximum, scores), axis=1, keepdims=True)
            total = None
            for score, (slot, _) in zip(scores, blocks):
                weights = jnp.exp2(score - peak).astype(jnp.bfloat16)
                value = jnp.where(mask, kv[slot, 1, :, columns(g)], jnp.ones((), jnp.bfloat16))
                term = jnp.dot(weights, value, preferred_element_type=jnp.float32)
                total = term if total is None else total + term
            totals.append(total)
            peaks.append(peak)
        top = jnp.where(first, totals[0], totals[1])
        low = pltpu.roll(jnp.where(first, totals[1], totals[0]), HD, 1)
        return top, low, jnp.where(first, peaks[0], peaks[1])

    def merged(g, part):
        top, low, peak = part
        best = jnp.maximum(peak, state[g, 2])
        new, old = jnp.exp2(peak - best), jnp.exp2(state[g, 2] - best)
        return top * new + state[g, 0] * old, low * new + state[g, 1] * old, best

    def keep(g, part):
        for i, value in enumerate(part):
            state[g, i] = value

    def at_start(g, chunks, act):
        for i, (start, _) in enumerate(chunks):
            @pl.when(g == start)
            def _():
                act(i)

    def relay(i):
        start, count = own_chunks[i]
        for stream in range(2):
            arrived(near_slot[stream], own_chunks, i)
            for j, (inner, _) in enumerate(far_chunks):
                if start <= inner < start + count:
                    pass_on(near_slot[stream], far_slot[stream], far_chunks, j, target[stream])
            pass_on(near_slot[stream], sib_slot[stream], own_chunks, i, sib)
        for slot in (SIB, B_LOW, B_HIGH):
            arrived(slot, own_chunks, i)

    @pl.loop(0, groups)
    def _(g):
        at_start(g, own_chunks, relay)
        keep(g, attend(g, near))

    def share(j):
        for part in range(2):
            mine = far_slot[0]
            remote(kv.at[mine, part], mine, far_chunks[j], part, j, sib).wait_recv()
            remote(kv.at[mine, part], FAR, far_chunks[j], part, j, sib).start()

    shares = ((0,), (1, 2), (3,), (4, 5), (6,), (7,), (), ())

    def prepare(j):
        for ahead in shares[j]:
            share(ahead)
        arrived(far_slot[1], far_chunks, j)
        arrived(FAR, far_chunks, j)

    @pl.loop(0, groups)
    def _(g):
        at_start(g, far_chunks, prepare)
        top, low, _ = merged(g, attend(g, outer))
        out_ref[:, columns(g)] = (top / low).astype(out_ref.dtype)

    for slot, chunks in (
        (SIB, own_chunks), (near_slot[0], own_chunks), (near_slot[1], own_chunks),
        (B_LOW, own_chunks), (B_HIGH, own_chunks), (C_LOW, far_chunks), (C_HIGH, far_chunks),
        (FAR, far_chunks),
    ):
        for i in range(len(chunks)):
            for part in range(2):
                if slot is near_slot[0] and i == part == 0:
                    continue
                remote(kv.at[slot, part], slot, chunks[i], part, i, sib).wait_send()


def spans(groups, sizes):
    starts = [sum(sizes[:i]) for i in range(len(sizes))]
    result = [(a, n) for a, n in zip(starts, sizes) if a + n < groups]
    done = sum(n for _, n in result)
    return result + [(done, groups - done)]


def solution(mesh):
    ring = mesh.shape["seq"]

    def per_device(queries, key_rows, values, bias_tiles, buckets, slopes):
        rows, width = queries.shape
        groups = width // LANES
        return pl.pallas_call(
            functools.partial(kernel, ring),
            out_shape=pltpu.VMEM((rows, width), queries.dtype),
            in_specs=[pl.BlockSpec(memory_space=pl.ANY)] * 6,
            out_specs=pl.BlockSpec(memory_space=pltpu.VMEM),
            scratch_shapes=[
                pltpu.VMEM((9, 2, rows, width), jnp.bfloat16),
                pltpu.VMEM((rows, width), jnp.bfloat16),
                pltpu.VMEM(bias_tiles.shape, jnp.bfloat16),
                pltpu.VMEM((2 * WIN + 1, rows, rows), jnp.float32),
                pltpu.VMEM((groups, 3, rows, LANES), jnp.float32),
                pltpu.SMEM(buckets.shape, jnp.int32),
                pltpu.SMEM(slopes.shape, jnp.float32),
                pltpu.SemaphoreType.DMA((9, 2, 8)),
                pltpu.SemaphoreType.DMA((9, 2, 8)),
                pltpu.SemaphoreType.DMA((6,)),
            ],
            compiler_params=pltpu.CompilerParams(
                collective_id=0, has_side_effects=True, vmem_limit_bytes=56 << 20
            ),
        )(buckets, slopes, queries, key_rows, values, bias_tiles)

    return jax.shard_map(
        per_device,
        mesh=mesh,
        in_specs=(P(("batch", "seq"), None),) * 3 + (P(), P(), P()),
        out_specs=P(("batch", "seq"), None),
        check_vma=False,
    )
```

```python
import functools
import math

import jax
import jax.numpy as jnp
from jax import lax
from jax.experimental import pallas as pl
from jax.experimental.pallas import tpu as pltpu
from jax.sharding import PartitionSpec as P

MESH = pl.DeviceIdType.MESH
HD = 64
WIN = 4
LANES = 128
LOG2E = math.log2(math.e)

OWN, SIB, A_LOW, A_HIGH, B_LOW, B_HIGH, C_LOW, C_HIGH, FAR = range(9)


def kernel(
    ring, buckets_hbm, slopes_hbm, q_hbm, k_hbm, v_hbm, tiles_hbm, out_ref,
    kv, q_buf, tiles, bias, state, sums, buckets, slopes, send_sem, recv_sem, in_sem, lead_sem,
):
    groups = q_buf.shape[1] // LANES
    me = lax.axis_index("seq")
    core = lax.rem(me, 2)
    up = lax.rem(me + 2, ring)
    down = lax.rem(me + ring - 2, ring)
    sib = me + 1 - 2 * core
    own_chunks = spans(groups, (4, 4, 4))
    far_chunks = spans(groups, (4, 4, 2, 2, 1, 1, 1))
    target = (lax.rem(me + ring - 2 + 4 * core, ring), lax.rem(me + 2 + ring - 4 * core, ring))
    near_slot = (A_HIGH - core, A_LOW + core)
    sib_slot = (B_HIGH - core, B_LOW + core)
    far_slot = (C_HIGH - core, C_LOW + core)

    def columns(g, count=1):
        return pl.ds(pl.multiple_of(g * LANES, LANES), count * LANES)

    def remote(src, dst, send, recv, device):
        return pltpu.make_async_remote_copy(
            src_ref=src, dst_ref=dst, send_sem=send, recv_sem=recv,
            device_id={"seq": device}, device_id_type=MESH,
        )

    def send_own(i, slot, device, first_sem=None):
        for part, ref in enumerate((k_hbm, v_hbm)):
            span = columns(*own_chunks[i])
            send = send_sem.at[slot, i] if first_sem is None or part else first_sem
            remote(
                ref.at[:, span], kv.at[slot, part, :, span], send, recv_sem.at[slot, i], device
            ).start()

    def passing(src, slot, chunks, i, device):
        span = columns(*chunks[i])
        return remote(
            kv.at[src, :, :, span], kv.at[slot, :, :, span],
            send_sem.at[slot, i], recv_sem.at[slot, i], device,
        )

    def arrived(slot, chunks, i):
        passing(slot, slot, chunks, i, sib).wait_recv()

    def left(slot, chunks, i):
        passing(slot, slot, chunks, i, sib).wait_send()

    def signal(semaphore, device):
        pl.semaphore_signal(semaphore, inc=1, device_id={"seq": device}, device_id_type=MESH)

    loads = [
        pltpu.make_async_copy(src, dst, in_sem.at[i])
        for i, (src, dst) in enumerate((
            (buckets_hbm, buckets), (tiles_hbm, tiles), (slopes_hbm, slopes), (q_hbm, q_buf),
            (k_hbm, kv.at[OWN, 0]), (v_hbm, kv.at[OWN, 1]),
        ))
    ]
    barrier = pltpu.get_barrier_semaphore()
    for device in (up, down, sib):
        signal(barrier, device)
    for load in loads:
        load.start()
    pl.semaphore_wait(barrier, 3)

    def start_stream(stream):
        for i in range(len(own_chunks)):
            send_own(
                i, near_slot[stream], target[stream], lead_sem if i == stream == 0 else None
            )

    start_stream(0)
    for i in range(len(own_chunks)):
        send_own(i, SIB, sib)

    loads[0].wait()
    loads[1].wait()
    for o in range(WIN + 1):
        tile = tiles[buckets[o]].astype(jnp.float32)
        bias[WIN + o] = tile.T
        if o > 0:
            bias[WIN - o] = tile

    head = columns(*own_chunks[0])
    remote(
        k_hbm.at[:, head], kv.at[OWN, 0, :, head], lead_sem, recv_sem.at[OWN, 0], sib
    ).wait_send()
    start_stream(1)
    for load in loads[2:]:
        load.wait()

    lane_head = lax.broadcasted_iota(jnp.int32, (1, LANES), 1) // HD
    near = (
        (OWN, 0), (SIB, 1 - 2 * core), (A_LOW, -2), (A_HIGH, 2),
        (B_LOW, -1 - 2 * core), (B_HIGH, 3 - 2 * core),
    )
    outer = ((C_LOW, -4), (C_HIGH, 4), (FAR, 6 * core - 3))

    def attend(g, blocks):
        query = q_buf[:, columns(g)] * jnp.asarray(HD ** -0.5, jnp.bfloat16)
        totals, peaks = [], []
        for half in range(2):
            mask = lane_head == half
            chosen = jnp.where(mask, query, jnp.zeros((), jnp.bfloat16))
            slope = slopes[2 * g + half] * LOG2E
            scores = []
            for slot, offset in blocks:
                dots = lax.dot_general(
                    kv[slot, 0, :, columns(g)], chosen, (((1,), (1,)), ((), ())),
                    preferred_element_type=jnp.float32,
                )
                scores.append(dots * LOG2E + slope * bias[offset + WIN])
            peak = jnp.max(functools.reduce(jnp.maximum, scores), axis=0, keepdims=True)
            total = None
            for score, (slot, _) in zip(scores, blocks):
                weights = jnp.exp2(score - peak).astype(jnp.bfloat16)
                value = jnp.where(mask, kv[slot, 1, :, columns(g)], jnp.ones((), jnp.bfloat16))
                term = lax.dot_general(
                    value, weights, (((0,), (0,)), ((), ())), preferred_element_type=jnp.float32
                )
                total = term if total is None else total + term
            totals.append(total)
            peaks.append(peak)
        tops = totals[0][:HD], totals[1][HD:]
        lows = totals[0][HD : HD + 1], totals[1][:1]
        return tops, lows, peaks

    def keep(g, part):
        tops, lows, peaks = part
        for half in range(2):
            state[g, half * HD : (half + 1) * HD] = tops[half]
            sums[g, half : half + 1] = lows[half]
            sums[g, half + 2 : half + 3] = peaks[half]

    def finish(g, part):
        tops, lows, peaks = part
        results = []
        for half in range(2):
            old_peak = sums[g, half + 2 : half + 3]
            best = jnp.maximum(peaks[half], old_peak)
            new, old = jnp.exp2(peaks[half] - best), jnp.exp2(old_peak - best)
            low = lows[half] * new + sums[g, half : half + 1] * old
            top = tops[half] * new + state[g, half * HD : (half + 1) * HD] * old
            results.append(top / low)
        out_ref[:, columns(g)] = jnp.concatenate(results, axis=0).T.astype(out_ref.dtype)

    def at_start(g, chunks, act):
        for i, (start, _) in enumerate(chunks):
            @pl.when(g == start)
            def _():
                act(i)

    def relay(i):
        start, count = own_chunks[i]
        for stream in range(2):
            arrived(near_slot[stream], own_chunks, i)
            for j, (inner, _) in enumerate(far_chunks):
                if start <= inner < start + count:
                    passing(
                        near_slot[stream], far_slot[stream], far_chunks, j, target[stream]
                    ).start()
            passing(near_slot[stream], sib_slot[stream], own_chunks, i, sib).start()
        for slot in (SIB, B_LOW, B_HIGH):
            arrived(slot, own_chunks, i)

    @pl.loop(0, groups)
    def _(g):
        at_start(g, own_chunks, relay)
        keep(g, attend(g, near))

    def share(j):
        arrived(far_slot[0], far_chunks, j)
        passing(far_slot[0], FAR, far_chunks, j, sib).start()

    for i in range(len(own_chunks)):
        for slot in (SIB, near_slot[1], B_LOW, B_HIGH):
            left(slot, own_chunks, i)
        if i > 0:
            left(near_slot[0], own_chunks, i)
    remote(
        v_hbm.at[:, head], kv.at[OWN, 1, :, head],
        send_sem.at[near_slot[0], 0], recv_sem.at[OWN, 0], sib,
    ).wait_send()

    shares = ((0,), (1, 2), (3,), (4, 5), (6,), (7,), (), ())

    def prepare(j):
        for ahead in shares[j]:
            share(ahead)
        arrived(far_slot[1], far_chunks, j)
        arrived(FAR, far_chunks, j)
        if j > 0:
            for slot in (C_LOW, C_HIGH, FAR):
                left(slot, far_chunks, j - 1)

    @pl.loop(0, groups)
    def _(g):
        at_start(g, far_chunks, prepare)
        finish(g, attend(g, outer))

    for slot in (C_LOW, C_HIGH, FAR):
        left(slot, far_chunks, len(far_chunks) - 1)


def spans(groups, sizes):
    starts = [sum(sizes[:i]) for i in range(len(sizes))]
    result = [(a, n) for a, n in zip(starts, sizes) if a + n < groups]
    done = sum(n for _, n in result)
    return result + [(done, groups - done)]


def solution(mesh):
    ring = mesh.shape["seq"]

    def per_device(queries, key_rows, values, bias_tiles, buckets, slopes):
        rows, width = queries.shape
        groups = width // LANES
        return pl.pallas_call(
            functools.partial(kernel, ring),
            out_shape=pltpu.VMEM((rows, width), queries.dtype),
            in_specs=[pl.BlockSpec(memory_space=pl.ANY)] * 6,
            out_specs=pl.BlockSpec(memory_space=pltpu.VMEM),
            scratch_shapes=[
                pltpu.VMEM((9, 2, rows, width), jnp.bfloat16),
                pltpu.VMEM((rows, width), jnp.bfloat16),
                pltpu.VMEM(bias_tiles.shape, jnp.bfloat16),
                pltpu.VMEM((2 * WIN + 1, rows, rows), jnp.float32),
                pltpu.VMEM((groups, LANES, rows), jnp.float32),
                pltpu.VMEM((groups, 8, rows), jnp.float32),
                pltpu.SMEM(buckets.shape, jnp.int32),
                pltpu.SMEM(slopes.shape, jnp.float32),
                pltpu.SemaphoreType.DMA((9, 8)),
                pltpu.SemaphoreType.DMA((9, 8)),
                pltpu.SemaphoreType.DMA((6,)),
                pltpu.SemaphoreType.DMA,
            ],
            compiler_params=pltpu.CompilerParams(
                collective_id=0, has_side_effects=True, vmem_limit_bytes=56 << 20
            ),
        )(buckets, slopes, queries, key_rows, values, bias_tiles)

    return jax.shard_map(
        per_device,
        mesh=mesh,
        in_specs=(P(("batch", "seq"), None),) * 3 + (P(), P(), P()),
        out_specs=P(("batch", "seq"), None),
        check_vma=False,
    )
```

```python
import functools
import math

import jax
import jax.numpy as jnp
from jax import lax
from jax.experimental import pallas as pl
from jax.experimental.pallas import tpu as pltpu
from jax.sharding import PartitionSpec as P

MESH = pl.DeviceIdType.MESH
HD = 64
WIN = 4
LANES = 128
LOG2E = math.log2(math.e)

OWN, SIB, A_LOW, A_HIGH, B_LOW, B_HIGH, C_LOW, C_HIGH, FAR = range(9)


def kernel(
    ring, buckets_hbm, slopes_hbm, q_hbm, k_hbm, v_hbm, tiles_hbm, out_ref,
    kv, q_buf, tiles, bias, state, sums, buckets, slopes, send_sem, near_sem, far_sem, in_sem, lead_sem,
):
    groups = q_buf.shape[1] // LANES
    me = lax.axis_index("seq")
    core = lax.rem(me, 2)
    up = lax.rem(me + 2, ring)
    down = lax.rem(me + ring - 2, ring)
    sib = me + 1 - 2 * core
    own_chunks = spans(groups, (2, 2, 4, 4))
    far_chunks = spans(groups, (2, 2, 4, 2, 2, 1, 1, 1))
    target = (lax.rem(me + ring - 2 + 4 * core, ring), lax.rem(me + 2 + ring - 4 * core, ring))
    near_slot = (A_HIGH - core, A_LOW + core)
    sib_slot = (B_HIGH - core, B_LOW + core)
    far_slot = (C_HIGH - core, C_LOW + core)

    def columns(g, count=1):
        return pl.ds(pl.multiple_of(g * LANES, LANES), count * LANES)

    def remote(src, dst, send, recv, device):
        return pltpu.make_async_remote_copy(
            src_ref=src, dst_ref=dst, send_sem=send, recv_sem=recv,
            device_id={"seq": device}, device_id_type=MESH,
        )

    def recv_sem(slot, chunks, i):
        return near_sem.at[slot - SIB, i] if chunks is own_chunks else far_sem.at[slot - C_LOW, i]

    def send_own(i, slot, device, first_sem=None):
        for part, ref in enumerate((k_hbm, v_hbm)):
            span = columns(*own_chunks[i])
            send = send_sem.at[slot] if first_sem is None or part else first_sem
            remote(
                ref.at[:, span], kv.at[slot, part, :, span],
                send, recv_sem(slot, own_chunks, i), device,
            ).start()

    def passing(src, slot, chunks, i, device):
        span = columns(*chunks[i])
        return remote(
            kv.at[src, :, :, span], kv.at[slot, :, :, span],
            send_sem.at[slot], recv_sem(slot, chunks, i), device,
        )

    def arrived(slot, chunks, i):
        passing(slot, slot, chunks, i, sib).wait_recv()

    def left(slot, count=None):
        whole = kv.at[slot, :, :, : (count or groups) * LANES]
        remote(whole, whole, send_sem.at[slot], near_sem.at[0, 0], sib).wait_send()

    def signal(semaphore, device):
        pl.semaphore_signal(semaphore, inc=1, device_id={"seq": device}, device_id_type=MESH)

    loads = [
        pltpu.make_async_copy(src, dst, in_sem.at[i])
        for i, (src, dst) in enumerate((
            (buckets_hbm, buckets), (tiles_hbm, tiles), (slopes_hbm, slopes), (q_hbm, q_buf),
            (k_hbm, kv.at[OWN, 0]), (v_hbm, kv.at[OWN, 1]),
        ))
    ]
    barrier = pltpu.get_barrier_semaphore()
    for device in (up, down, sib):
        signal(barrier, device)
    for load in loads:
        load.start()
    pl.semaphore_wait(barrier, 3)

    def start_stream(stream):
        for i in range(len(own_chunks)):
            send_own(
                i, near_slot[stream], target[stream], lead_sem if i == stream == 0 else None
            )

    start_stream(0)
    for i in range(len(own_chunks)):
        send_own(i, SIB, sib)

    loads[0].wait()
    loads[1].wait()
    for o in range(WIN + 1):
        tile = tiles[buckets[o]].astype(jnp.float32)
        bias[WIN + o] = tile.T
        if o > 0:
            bias[WIN - o] = tile

    head = columns(*own_chunks[0])
    remote(
        k_hbm.at[:, head], kv.at[OWN, 0, :, head], lead_sem, near_sem.at[0, 0], sib
    ).wait_send()
    start_stream(1)
    for load in loads[2:]:
        load.wait()

    lane_head = lax.broadcasted_iota(jnp.int32, (1, LANES), 1) // HD
    near = (
        (OWN, 0), (SIB, 1 - 2 * core), (A_LOW, -2), (A_HIGH, 2),
        (B_LOW, -1 - 2 * core), (B_HIGH, 3 - 2 * core),
    )
    outer = ((C_LOW, -4), (C_HIGH, 4), (FAR, 6 * core - 3))

    def attend(g, blocks):
        query = q_buf[:, columns(g)] * jnp.asarray(HD ** -0.5, jnp.bfloat16)
        totals, peaks = [], []
        for half in range(2):
            mask = lane_head == half
            chosen = jnp.where(mask, query, jnp.zeros((), jnp.bfloat16))
            slope = slopes[2 * g + half] * LOG2E
            scores = []
            for slot, offset in blocks:
                dots = lax.dot_general(
                    kv[slot, 0, :, columns(g)], chosen, (((1,), (1,)), ((), ())),
                    preferred_element_type=jnp.float32,
                )
                scores.append(dots * LOG2E + slope * bias[offset + WIN])
            peak = jnp.max(functools.reduce(jnp.maximum, scores), axis=0, keepdims=True)
            total = None
            for score, (slot, _) in zip(scores, blocks):
                weights = jnp.exp2(score - peak).astype(jnp.bfloat16)
                value = jnp.where(mask, kv[slot, 1, :, columns(g)], jnp.ones((), jnp.bfloat16))
                term = lax.dot_general(
                    value, weights, (((0,), (0,)), ((), ())), preferred_element_type=jnp.float32
                )
                total = term if total is None else total + term
            totals.append(total)
            peaks.append(peak)
        tops = totals[0][:HD], totals[1][HD:]
        lows = totals[0][HD : HD + 1], totals[1][:1]
        return tops, lows, peaks

    def keep(g, part):
        tops, lows, peaks = part
        for half in range(2):
            state[g, half * HD : (half + 1) * HD] = tops[half]
            sums[g, half : half + 1] = lows[half]
            sums[g, half + 2 : half + 3] = peaks[half]

    def finish(g, part):
        tops, lows, peaks = part
        results = []
        for half in range(2):
            old_peak = sums[g, half + 2 : half + 3]
            best = jnp.maximum(peaks[half], old_peak)
            new, old = jnp.exp2(peaks[half] - best), jnp.exp2(old_peak - best)
            low = lows[half] * new + sums[g, half : half + 1] * old
            top = tops[half] * new + state[g, half * HD : (half + 1) * HD] * old
            results.append(top / low)
        out_ref[:, columns(g)] = jnp.concatenate(results, axis=0).T.astype(out_ref.dtype)

    def at_start(g, chunks, act):
        for i, (start, _) in enumerate(chunks):
            @pl.when(g == start)
            def _():
                act(i)

    def relay(i):
        start, count = own_chunks[i]
        for stream in range(2):
            arrived(near_slot[stream], own_chunks, i)
            for j, (inner, _) in enumerate(far_chunks):
                if start <= inner < start + count:
                    passing(
                        near_slot[stream], far_slot[stream], far_chunks, j, target[stream]
                    ).start()
            passing(near_slot[stream], sib_slot[stream], own_chunks, i, sib).start()
        for slot in (SIB, B_LOW, B_HIGH):
            arrived(slot, own_chunks, i)

    @pl.loop(0, groups)
    def _(g):
        at_start(g, own_chunks, relay)
        keep(g, attend(g, near))

    def share(j):
        arrived(far_slot[0], far_chunks, j)
        passing(far_slot[0], FAR, far_chunks, j, sib).start()

    for slot in (SIB, near_slot[1], B_LOW, B_HIGH):
        left(slot)
    left(near_slot[0], groups - own_chunks[0][1] // 2)

    shares = ((0,), (1,), (2, 3), (4,), (5, 6), (7,), (8,), (), ())

    def prepare(j):
        for ahead in shares[j]:
            share(ahead)
        arrived(far_slot[1], far_chunks, j)
        arrived(FAR, far_chunks, j)

    @pl.loop(0, groups)
    def _(g):
        at_start(g, far_chunks, prepare)
        finish(g, attend(g, outer))

    for slot in (C_LOW, C_HIGH, FAR):
        left(slot)


def spans(groups, sizes):
    starts = [sum(sizes[:i]) for i in range(len(sizes))]
    result = [(a, n) for a, n in zip(starts, sizes) if a + n < groups]
    done = sum(n for _, n in result)
    return result + [(done, groups - done)]


def solution(mesh):
    ring = mesh.shape["seq"]

    def per_device(queries, key_rows, values, bias_tiles, buckets, slopes):
        rows, width = queries.shape
        groups = width // LANES
        return pl.pallas_call(
            functools.partial(kernel, ring),
            out_shape=pltpu.VMEM((rows, width), queries.dtype),
            in_specs=[pl.BlockSpec(memory_space=pl.ANY)] * 6,
            out_specs=pl.BlockSpec(memory_space=pltpu.VMEM),
            scratch_shapes=[
                pltpu.VMEM((9, 2, rows, width), jnp.bfloat16),
                pltpu.VMEM((rows, width), jnp.bfloat16),
                pltpu.VMEM(bias_tiles.shape, jnp.bfloat16),
                pltpu.VMEM((2 * WIN + 1, rows, rows), jnp.float32),
                pltpu.VMEM((groups, LANES, rows), jnp.float32),
                pltpu.VMEM((groups, 8, rows), jnp.float32),
                pltpu.SMEM(buckets.shape, jnp.int32),
                pltpu.SMEM(slopes.shape, jnp.float32),
                pltpu.SemaphoreType.DMA((9,)),
                pltpu.SemaphoreType.DMA((5, 5)),
                pltpu.SemaphoreType.DMA((3, 9)),
                pltpu.SemaphoreType.DMA((6,)),
                pltpu.SemaphoreType.DMA,
            ],
            compiler_params=pltpu.CompilerParams(
                collective_id=0, has_side_effects=True, vmem_limit_bytes=56 << 20
            ),
        )(buckets, slopes, queries, key_rows, values, bias_tiles)

    return jax.shard_map(
        per_device,
        mesh=mesh,
        in_specs=(P(("batch", "seq"), None),) * 3 + (P(), P(), P()),
        out_specs=P(("batch", "seq"), None),
        check_vma=False,
    )
```

```python
import functools
import math

import jax
import jax.numpy as jnp
from jax import lax
from jax.experimental import pallas as pl
from jax.experimental.pallas import tpu as pltpu
from jax.sharding import PartitionSpec as P

MESH = pl.DeviceIdType.MESH
HD = 64
WIN = 4
LANES = 128
LOG2E = math.log2(math.e)

OWN, SIB, A_LOW, A_HIGH, B_LOW, B_HIGH, C_LOW, C_HIGH, FAR = range(9)


def kernel(
    ring, buckets_hbm, slopes_hbm, q_hbm, k_hbm, v_hbm, tiles_hbm, out_ref,
    kv, q_buf, tiles, bias, state, sums, buckets, slopes, send_sem, near_sem, far_sem, in_sem, lead_sem,
):
    groups = q_buf.shape[1] // LANES
    me = lax.axis_index("seq")
    core = lax.rem(me, 2)
    up = lax.rem(me + 2, ring)
    down = lax.rem(me + ring - 2, ring)
    sib = me + 1 - 2 * core
    own_chunks = spans(groups, (2, 2, 4, 4))
    far_chunks = spans(groups, (2, 2, 4, 2, 2, 1, 1, 1))
    last = len(far_chunks) - 1
    target = (lax.rem(me + ring - 2 + 4 * core, ring), lax.rem(me + 2 + ring - 4 * core, ring))
    near_slot = (A_HIGH - core, A_LOW + core)
    sib_slot = (B_HIGH - core, B_LOW + core)
    far_slot = (C_HIGH - core, C_LOW + core)

    def columns(g, count=1):
        return pl.ds(pl.multiple_of(g * LANES, LANES), count * LANES)

    def remote(src, dst, send, recv, device):
        return pltpu.make_async_remote_copy(
            src_ref=src, dst_ref=dst, send_sem=send, recv_sem=recv,
            device_id={"seq": device}, device_id_type=MESH,
        )

    def recv_sem(slot, chunks, i):
        return near_sem.at[slot - SIB, i] if chunks is own_chunks else far_sem.at[slot - C_LOW, i]

    def send_own(i, slot, device, first_sem=None):
        for part, ref in enumerate((k_hbm, v_hbm)):
            span = columns(*own_chunks[i])
            send = send_sem.at[slot] if first_sem is None or part else first_sem
            remote(
                ref.at[:, span], kv.at[slot, part, :, span],
                send, recv_sem(slot, own_chunks, i), device,
            ).start()

    def passing(src, slot, chunks, i, device):
        span = columns(*chunks[i])
        return remote(
            kv.at[src, :, :, span], kv.at[slot, :, :, span],
            send_sem.at[slot], recv_sem(slot, chunks, i), device,
        )

    def final(src, slot, part, device):
        span = columns(*far_chunks[last])
        return remote(
            kv.at[src, part, :, span], kv.at[slot, part, :, span],
            send_sem.at[slot], far_sem.at[slot - C_LOW, last + part], device,
        )

    def arrived(slot, chunks, i):
        passing(slot, slot, chunks, i, sib).wait_recv()

    def left(slot, count=None):
        whole = kv.at[slot, :, :, : (count or groups) * LANES]
        remote(whole, whole, send_sem.at[slot], near_sem.at[0, 0], sib).wait_send()

    def signal(semaphore, device):
        pl.semaphore_signal(semaphore, inc=1, device_id={"seq": device}, device_id_type=MESH)

    loads = [
        pltpu.make_async_copy(src, dst, in_sem.at[i])
        for i, (src, dst) in enumerate((
            (buckets_hbm, buckets), (tiles_hbm, tiles), (slopes_hbm, slopes), (q_hbm, q_buf),
            (k_hbm, kv.at[OWN, 0]), (v_hbm, kv.at[OWN, 1]),
        ))
    ]
    barrier = pltpu.get_barrier_semaphore()
    for device in (up, down, sib):
        signal(barrier, device)
    for load in loads:
        load.start()
    pl.semaphore_wait(barrier, 3)

    def start_stream(stream):
        for i in range(len(own_chunks)):
            send_own(
                i, near_slot[stream], target[stream], lead_sem if i == stream == 0 else None
            )

    start_stream(0)
    for i in range(len(own_chunks)):
        send_own(i, SIB, sib)

    loads[0].wait()
    loads[1].wait()
    for o in range(WIN + 1):
        tile = tiles[buckets[o]].astype(jnp.float32)
        bias[WIN + o] = tile.T
        if o > 0:
            bias[WIN - o] = tile

    head = columns(*own_chunks[0])
    remote(
        k_hbm.at[:, head], kv.at[OWN, 0, :, head], lead_sem, near_sem.at[0, 0], sib
    ).wait_send()
    start_stream(1)
    for load in loads[2:]:
        load.wait()

    lane_head = lax.broadcasted_iota(jnp.int32, (1, LANES), 1) // HD
    near = (
        (OWN, 0), (SIB, 1 - 2 * core), (A_LOW, -2), (A_HIGH, 2),
        (B_LOW, -1 - 2 * core), (B_HIGH, 3 - 2 * core),
    )
    outer = ((C_LOW, -4), (C_HIGH, 4), (FAR, 6 * core - 3))

    def attend(g, blocks, values_here=None):
        query = q_buf[:, columns(g)] * jnp.asarray(HD ** -0.5, jnp.bfloat16)
        weights, totals, peaks = [], [], []
        for half in range(2):
            chosen = jnp.where(lane_head == half, query, jnp.zeros((), jnp.bfloat16))
            slope = slopes[2 * g + half] * LOG2E
            scores = []
            for slot, offset in blocks:
                dots = lax.dot_general(
                    kv[slot, 0, :, columns(g)], chosen, (((1,), (1,)), ((), ())),
                    preferred_element_type=jnp.float32,
                )
                scores.append(dots * LOG2E + slope * bias[offset + WIN])
            peak = jnp.max(functools.reduce(jnp.maximum, scores), axis=0, keepdims=True)
            weights.append([jnp.exp2(score - peak).astype(jnp.bfloat16) for score in scores])
            peaks.append(peak)
        if values_here is not None:
            values_here()
        for half in range(2):
            total = None
            for weight, (slot, _) in zip(weights[half], blocks):
                value = jnp.where(
                    lane_head == half, kv[slot, 1, :, columns(g)], jnp.ones((), jnp.bfloat16)
                )
                term = lax.dot_general(
                    value, weight, (((0,), (0,)), ((), ())), preferred_element_type=jnp.float32
                )
                total = term if total is None else total + term
            totals.append(total)
        tops = totals[0][:HD], totals[1][HD:]
        lows = totals[0][HD : HD + 1], totals[1][:1]
        return tops, lows, peaks

    def keep(g, part):
        tops, lows, peaks = part
        for half in range(2):
            state[g, half * HD : (half + 1) * HD] = tops[half]
            sums[g, half : half + 1] = lows[half]
            sums[g, half + 2 : half + 3] = peaks[half]

    def finish(g, part):
        tops, lows, peaks = part
        results = []
        for half in range(2):
            old_peak = sums[g, half + 2 : half + 3]
            best = jnp.maximum(peaks[half], old_peak)
            new, old = jnp.exp2(peaks[half] - best), jnp.exp2(old_peak - best)
            low = lows[half] * new + sums[g, half : half + 1] * old
            top = tops[half] * new + state[g, half * HD : (half + 1) * HD] * old
            results.append(top / low)
        out_ref[:, columns(g)] = jnp.concatenate(results, axis=0).T.astype(out_ref.dtype)

    def at_start(g, chunks, act):
        for i, (start, _) in enumerate(chunks):
            @pl.when(g == start)
            def _():
                act(i)

    def relay(i):
        start, count = own_chunks[i]
        for stream in range(2):
            arrived(near_slot[stream], own_chunks, i)
            for j, (inner, _) in enumerate(far_chunks):
                if start <= inner < start + count:
                    if j == last:
                        for part in range(2):
                            final(
                                near_slot[stream], far_slot[stream], part, target[stream]
                            ).start()
                        continue
                    passing(
                        near_slot[stream], far_slot[stream], far_chunks, j, target[stream]
                    ).start()
            passing(near_slot[stream], sib_slot[stream], own_chunks, i, sib).start()
        for slot in (SIB, B_LOW, B_HIGH):
            arrived(slot, own_chunks, i)

    @pl.loop(0, groups)
    def _(g):
        at_start(g, own_chunks, relay)
        keep(g, attend(g, near))

    def share(j):
        arrived(far_slot[0], far_chunks, j)
        passing(far_slot[0], FAR, far_chunks, j, sib).start()

    for slot in (SIB, near_slot[1], B_LOW, B_HIGH):
        left(slot)
    left(near_slot[0], groups - own_chunks[0][1] // 2)

    shares = ((0,), (1,), (2, 3), (4,), (5, 6), (7,), (8,), (), ())

    def prepare(j):
        for ahead in shares[j]:
            if ahead < last:
                share(ahead)
        arrived(far_slot[1], far_chunks, j)
        arrived(FAR, far_chunks, j)
        if last in shares[j]:
            share_last()

    def share_last():
        for part in range(2):
            final(far_slot[0], far_slot[0], part, sib).wait_recv()
            final(far_slot[0], FAR, part, sib).start()

    def here(part):
        final(far_slot[1], far_slot[1], part, sib).wait_recv()
        final(FAR, FAR, part, sib).wait_recv()

    @pl.loop(0, groups - 1)
    def _(g):
        at_start(g, far_chunks[:last], prepare)
        finish(g, attend(g, outer))

    here(0)
    finish(groups - 1, attend(groups - 1, outer, lambda: here(1)))

    for slot in (C_LOW, C_HIGH, FAR):
        left(slot)


def spans(groups, sizes):
    starts = [sum(sizes[:i]) for i in range(len(sizes))]
    result = [(a, n) for a, n in zip(starts, sizes) if a + n < groups]
    done = sum(n for _, n in result)
    return result + [(done, groups - done)]


def solution(mesh):
    ring = mesh.shape["seq"]

    def per_device(queries, key_rows, values, bias_tiles, buckets, slopes):
        rows, width = queries.shape
        groups = width // LANES
        return pl.pallas_call(
            functools.partial(kernel, ring),
            out_shape=pltpu.VMEM((rows, width), queries.dtype),
            in_specs=[pl.BlockSpec(memory_space=pl.ANY)] * 6,
            out_specs=pl.BlockSpec(memory_space=pltpu.VMEM),
            scratch_shapes=[
                pltpu.VMEM((9, 2, rows, width), jnp.bfloat16),
                pltpu.VMEM((rows, width), jnp.bfloat16),
                pltpu.VMEM(bias_tiles.shape, jnp.bfloat16),
                pltpu.VMEM((2 * WIN + 1, rows, rows), jnp.float32),
                pltpu.VMEM((groups, LANES, rows), jnp.float32),
                pltpu.VMEM((groups, 8, rows), jnp.float32),
                pltpu.SMEM(buckets.shape, jnp.int32),
                pltpu.SMEM(slopes.shape, jnp.float32),
                pltpu.SemaphoreType.DMA((9,)),
                pltpu.SemaphoreType.DMA((5, 5)),
                pltpu.SemaphoreType.DMA((3, 10)),
                pltpu.SemaphoreType.DMA((6,)),
                pltpu.SemaphoreType.DMA,
            ],
            compiler_params=pltpu.CompilerParams(
                collective_id=0, has_side_effects=True, vmem_limit_bytes=56 << 20
            ),
        )(buckets, slopes, queries, key_rows, values, bias_tiles)

    return jax.shard_map(
        per_device,
        mesh=mesh,
        in_specs=(P(("batch", "seq"), None),) * 3 + (P(), P(), P()),
        out_specs=P(("batch", "seq"), None),
        check_vma=False,
    )
```

```python
import functools
import math

import jax
import jax.numpy as jnp
from jax import lax
from jax.experimental import pallas as pl
from jax.experimental.pallas import tpu as pltpu
from jax.sharding import PartitionSpec as P

MESH = pl.DeviceIdType.MESH
HD = 64
WIN = 4
LANES = 128
LOG2E = math.log2(math.e)

OWN, SIB, A_LOW, A_HIGH, B_LOW, B_HIGH, C_LOW, C_HIGH, FAR = range(9)


def kernel(
    ring, buckets_hbm, slopes_hbm, q_hbm, k_hbm, v_hbm, tiles_hbm, out_ref,
    kv, q_buf, tiles, bias, state, sums, buckets, slopes, send_sem, near_sem, far_sem, in_sem, lead_sem, sib_sem,
):
    groups = q_buf.shape[1] // LANES
    me = lax.axis_index("seq")
    core = lax.rem(me, 2)
    up = lax.rem(me + 2, ring)
    down = lax.rem(me + ring - 2, ring)
    sib = me + 1 - 2 * core
    own_chunks = spans(groups, (2, 2, 4, 4))
    far_chunks = spans(groups, (2, 2, 4, 2, 2, 1, 1, 1))
    last = len(far_chunks) - 1
    target = (lax.rem(me + ring - 2 + 4 * core, ring), lax.rem(me + 2 + ring - 4 * core, ring))
    near_slot = (A_HIGH - core, A_LOW + core)
    sib_slot = (B_HIGH - core, B_LOW + core)
    far_slot = (C_HIGH - core, C_LOW + core)

    def columns(g, count=1):
        return pl.ds(pl.multiple_of(g * LANES, LANES), count * LANES)

    def remote(src, dst, send, recv, device):
        return pltpu.make_async_remote_copy(
            src_ref=src, dst_ref=dst, send_sem=send, recv_sem=recv,
            device_id={"seq": device}, device_id_type=MESH,
        )

    def recv_sem(slot, chunks, i):
        return near_sem.at[slot - A_LOW, i] if chunks is own_chunks else far_sem.at[slot - C_LOW, i]

    def send_own(i, slot, device, first_sem=None):
        for part, ref in enumerate((k_hbm, v_hbm)):
            span = columns(*own_chunks[i])
            send = send_sem.at[slot] if first_sem is None or part else first_sem
            remote(
                ref.at[:, span], kv.at[slot, part, :, span],
                send, recv_sem(slot, own_chunks, i), device,
            ).start()

    def passing(src, slot, chunks, i, device):
        span = columns(*chunks[i])
        return remote(
            kv.at[src, :, :, span], kv.at[slot, :, :, span],
            send_sem.at[slot], recv_sem(slot, chunks, i), device,
        )

    def final(src, slot, part, device):
        span = columns(*far_chunks[last])
        return remote(
            kv.at[src, part, :, span], kv.at[slot, part, :, span],
            send_sem.at[slot], far_sem.at[slot - C_LOW, last + part], device,
        )

    def arrived(slot, chunks, i):
        passing(slot, slot, chunks, i, sib).wait_recv()

    def left(slot, count=None):
        whole = kv.at[slot, :, :, : (count or groups) * LANES]
        remote(whole, whole, send_sem.at[slot], near_sem.at[0, 0], sib).wait_send()

    def signal(semaphore, device):
        pl.semaphore_signal(semaphore, inc=1, device_id={"seq": device}, device_id_type=MESH)

    loads = [
        pltpu.make_async_copy(src, dst, in_sem.at[i])
        for i, (src, dst) in enumerate((
            (buckets_hbm, buckets), (tiles_hbm, tiles), (slopes_hbm, slopes), (q_hbm, q_buf),
            (k_hbm, kv.at[OWN, 0]), (v_hbm, kv.at[OWN, 1]),
        ))
    ]
    barrier = pltpu.get_barrier_semaphore()
    for device in (up, down, sib):
        signal(barrier, device)
    for load in loads:
        load.start()
    pl.semaphore_wait(barrier, 3)

    def start_stream(stream):
        for i in range(len(own_chunks)):
            send_own(
                i, near_slot[stream], target[stream], lead_sem if i == stream == 0 else None
            )

    start_stream(0)
    for part, ref in enumerate((k_hbm, v_hbm)):
        remote(ref, kv.at[SIB, part], send_sem.at[SIB], sib_sem, sib).start()

    head = columns(*own_chunks[0])
    remote(
        k_hbm.at[:, head], kv.at[OWN, 0, :, head], lead_sem, near_sem.at[0, 0], sib
    ).wait_send()
    start_stream(1)

    loads[0].wait()
    loads[1].wait()
    for o in range(WIN + 1):
        tile = tiles[buckets[o]].astype(jnp.float32)
        bias[WIN + o] = tile.T
        if o > 0:
            bias[WIN - o] = tile

    for load in loads[2:]:
        load.wait()

    lane_head = lax.broadcasted_iota(jnp.int32, (1, LANES), 1) // HD
    near = (
        (OWN, 0), (SIB, 1 - 2 * core), (A_LOW, -2), (A_HIGH, 2),
        (B_LOW, -1 - 2 * core), (B_HIGH, 3 - 2 * core),
    )
    outer = ((C_LOW, -4), (C_HIGH, 4), (FAR, 6 * core - 3))

    def attend(g, blocks, values_here=None):
        query = q_buf[:, columns(g)] * jnp.asarray(HD ** -0.5, jnp.bfloat16)
        weights, totals, peaks = [], [], []
        for half in range(2):
            chosen = jnp.where(lane_head == half, query, jnp.zeros((), jnp.bfloat16))
            slope = slopes[2 * g + half] * LOG2E
            scores = []
            for slot, offset in blocks:
                dots = lax.dot_general(
                    kv[slot, 0, :, columns(g)], chosen, (((1,), (1,)), ((), ())),
                    preferred_element_type=jnp.float32,
                )
                scores.append(dots * LOG2E + slope * bias[offset + WIN])
            peak = jnp.max(functools.reduce(jnp.maximum, scores), axis=0, keepdims=True)
            weights.append([jnp.exp2(score - peak).astype(jnp.bfloat16) for score in scores])
            peaks.append(peak)
        if values_here is not None:
            values_here()
        for half in range(2):
            total = None
            for weight, (slot, _) in zip(weights[half], blocks):
                value = jnp.where(
                    lane_head == half, kv[slot, 1, :, columns(g)], jnp.ones((), jnp.bfloat16)
                )
                term = lax.dot_general(
                    value, weight, (((0,), (0,)), ((), ())), preferred_element_type=jnp.float32
                )
                total = term if total is None else total + term
            totals.append(total)
        tops = totals[0][:HD], totals[1][HD:]
        lows = totals[0][HD : HD + 1], totals[1][:1]
        return tops, lows, peaks

    def keep(g, part):
        tops, lows, peaks = part
        for half in range(2):
            state[g, half * HD : (half + 1) * HD] = tops[half]
            sums[g, half : half + 1] = lows[half]
            sums[g, half + 2 : half + 3] = peaks[half]

    def finish(g, part):
        tops, lows, peaks = part
        results = []
        for half in range(2):
            old_peak = sums[g, half + 2 : half + 3]
            best = jnp.maximum(peaks[half], old_peak)
            new, old = jnp.exp2(peaks[half] - best), jnp.exp2(old_peak - best)
            low = lows[half] * new + sums[g, half : half + 1] * old
            top = tops[half] * new + state[g, half * HD : (half + 1) * HD] * old
            results.append(top / low)
        out_ref[:, columns(g)] = jnp.concatenate(results, axis=0).T.astype(out_ref.dtype)

    def at_start(g, chunks, act):
        for i, (start, _) in enumerate(chunks):
            @pl.when(g == start)
            def _():
                act(i)

    def relay(i):
        start, count = own_chunks[i]
        for stream in range(2):
            arrived(near_slot[stream], own_chunks, i)
            for j, (inner, _) in enumerate(far_chunks):
                if start <= inner < start + count:
                    if j == last:
                        for part in range(2):
                            final(
                                near_slot[stream], far_slot[stream], part, target[stream]
                            ).start()
                        continue
                    passing(
                        near_slot[stream], far_slot[stream], far_chunks, j, target[stream]
                    ).start()
            passing(near_slot[stream], sib_slot[stream], own_chunks, i, sib).start()
        for slot in (B_LOW, B_HIGH):
            arrived(slot, own_chunks, i)
        if i == 0:
            remote(kv.at[SIB], kv.at[SIB], send_sem.at[SIB], sib_sem, sib).wait_recv()

    @pl.loop(0, groups)
    def _(g):
        at_start(g, own_chunks, relay)
        keep(g, attend(g, near))

    def share(j):
        arrived(far_slot[0], far_chunks, j)
        passing(far_slot[0], FAR, far_chunks, j, sib).start()

    for slot in (SIB, near_slot[1], B_LOW, B_HIGH):
        left(slot)
    left(near_slot[0], groups - own_chunks[0][1] // 2)

    shares = ((0,), (1,), (2, 3), (4,), (5, 6), (7,), (8,), (), ())

    def prepare(j):
        for ahead in shares[j]:
            if ahead < last:
                share(ahead)
        arrived(far_slot[1], far_chunks, j)
        arrived(FAR, far_chunks, j)
        if last in shares[j]:
            share_last()

    def share_last():
        for part in range(2):
            final(far_slot[0], far_slot[0], part, sib).wait_recv()
            final(far_slot[0], FAR, part, sib).start()

    def here(part):
        final(far_slot[1], far_slot[1], part, sib).wait_recv()
        final(FAR, FAR, part, sib).wait_recv()

    @pl.loop(0, groups - 1)
    def _(g):
        at_start(g, far_chunks[:last], prepare)
        finish(g, attend(g, outer))

    here(0)
    finish(groups - 1, attend(groups - 1, outer, lambda: here(1)))

    for slot in (C_LOW, C_HIGH, FAR):
        left(slot)


def spans(groups, sizes):
    starts = [sum(sizes[:i]) for i in range(len(sizes))]
    result = [(a, n) for a, n in zip(starts, sizes) if a + n < groups]
    done = sum(n for _, n in result)
    return result + [(done, groups - done)]


def solution(mesh):
    ring = mesh.shape["seq"]

    def per_device(queries, key_rows, values, bias_tiles, buckets, slopes):
        rows, width = queries.shape
        groups = width // LANES
        return pl.pallas_call(
            functools.partial(kernel, ring),
            out_shape=pltpu.VMEM((rows, width), queries.dtype),
            in_specs=[pl.BlockSpec(memory_space=pl.ANY)] * 6,
            out_specs=pl.BlockSpec(memory_space=pltpu.VMEM),
            scratch_shapes=[
                pltpu.VMEM((9, 2, rows, width), jnp.bfloat16),
                pltpu.VMEM((rows, width), jnp.bfloat16),
                pltpu.VMEM(bias_tiles.shape, jnp.bfloat16),
                pltpu.VMEM((2 * WIN + 1, rows, rows), jnp.float32),
                pltpu.VMEM((groups, LANES, rows), jnp.float32),
                pltpu.VMEM((groups, 8, rows), jnp.float32),
                pltpu.SMEM(buckets.shape, jnp.int32),
                pltpu.SMEM(slopes.shape, jnp.float32),
                pltpu.SemaphoreType.DMA((9,)),
                pltpu.SemaphoreType.DMA((4, 5)),
                pltpu.SemaphoreType.DMA((3, 10)),
                pltpu.SemaphoreType.DMA((6,)),
                pltpu.SemaphoreType.DMA,
                pltpu.SemaphoreType.DMA,
            ],
            compiler_params=pltpu.CompilerParams(
                collective_id=0, has_side_effects=True, vmem_limit_bytes=56 << 20
            ),
        )(buckets, slopes, queries, key_rows, values, bias_tiles)

    return jax.shard_map(
        per_device,
        mesh=mesh,
        in_specs=(P(("batch", "seq"), None),) * 3 + (P(), P(), P()),
        out_specs=P(("batch", "seq"), None),
        check_vma=False,
    )
```
